32 devices in a mesh: seq: 4 (over y, x), dp: 8 (over z, core).
Axes of the slice: x: 2, y: 2, z: 4, core: 2. Of those that a mesh axis runs over, the one named last changes fastest.
Arguments:
- stream: bfloat16 [8, 1024, 1024], P('dp', 'seq'), may hold values from -6 to 6
- cotangent: bfloat16 [8, 1024, 1024], P('dp', 'seq'), may hold values from -6 to 6
- domains: int32 [8], replicated, may hold values from 0 to 7
- lengths: int32 [8], replicated, may hold values from 1 to 1024, 6144 in all
- domain_weight: float32 [8], replicated, may hold values from 0.5 to 2
- in_master: float32 [1024, 1792], P(('seq', 'dp')), may hold values from -0.1875 to 0.1875
- in_first: float32 [1024, 1792], P(('seq', 'dp')), may hold values from -112 to 112
- in_second: float32 [1024, 1792], P(('seq', 'dp')), may hold values from 24.576 to 98.304
- out_master: float32 [4096, 1024], P(('seq', 'dp')), may hold values from -0.00390625 to 0.00390625
- out_first: float32 [4096, 1024], P(('seq', 'dp')), may hold values from -1024 to 1024
- out_second: float32 [4096, 1024], P(('seq', 'dp')), may hold values from 3145.728 to 12582.912
- gu_master: float32 [1024, 2, 2816], P('dp', None, 'seq'), may hold values from -0.1875 to 0.1875
- gu_first: float32 [1024, 2, 2816], P('dp', None, 'seq'), may hold values from -20 to 20
- gu_second: float32 [1024, 2, 2816], P('dp', None, 'seq'), may hold values from 0.98304 to 3.93216
- down_master: float32 [2816, 1024], P('seq', 'dp'), may hold values from -0.109375 to 0.109375
- down_first: float32 [2816, 1024], P('seq', 'dp'), may hold values from -32 to 32
- down_second: float32 [2816, 1024], P('seq', 'dp'), may hold values from 3.01056 to 12.04224
- gain_master: float32 [2, 1024], P(None, ('seq', 'dp')), may hold values from 0.5 to 1.5
- gain_first: float32 [2, 1024], P(None, ('seq', 'dp')), may hold values from -80 to 80
- gain_second: float32 [2, 1024], P(None, ('seq', 'dp')), may hold values from 13.824 to 55.296
- gate_bias: float32 [128], replicated, may hold values from -1 to 12
- bias_first: float32 [128], replicated, may hold values from -8 to 8
- bias_second: float32 [128], replicated, may hold values from 0.13824 to 0.55296
Outputs:
- output: bfloat16 [8, 1024, 1024], P('dp', 'seq')
- grad_stream: bfloat16 [8, 1024, 1024], P('dp', 'seq')
- in_weight_new: float32 [1024, 1792], P(('seq', 'dp'))
- in_first_new: float32 [1024, 1792], P(('seq', 'dp'))
- in_second_new: float32 [1024, 1792], P(('seq', 'dp'))
- out_weight_new: float32 [4096, 1024], P(('seq', 'dp'))
- out_first_new: float32 [4096, 1024], P(('seq', 'dp'))
- out_second_new: float32 [4096, 1024], P(('seq', 'dp'))
- gu_weight_new: float32 [1024, 2, 2816], P('dp', None, 'seq')
- gu_first_new: float32 [1024, 2, 2816], P('dp', None, 'seq')
- gu_second_new: float32 [1024, 2, 2816], P('dp', None, 'seq')
- down_weight_new: float32 [2816, 1024], P('seq', 'dp')
- down_first_new: float32 [2816, 1024], P('seq', 'dp')
- down_second_new: float32 [2816, 1024], P('seq', 'dp')
- gain_weight_new: float32 [2, 1024], P(None, ('seq', 'dp'))
- gain_first_new: float32 [2, 1024], P(None, ('seq', 'dp'))
- gain_second_new: float32 [2, 1024], P(None, ('seq', 'dp'))
- gate_bias_new: float32 [128], replicated
- bias_first_new: float32 [128], replicated
- bias_second_new: float32 [128], replicated
- norm_table: float32 [2, 11], replicated
- stream_stats: float32 [3], replicated
The draws below stay inside these ranges and needn't reach their ends.
Inputs may be any that keep to these rules, and one draw needn't show every extreme that they name: The first lengths[s] positions of sequence s are valid; some sequence is valid in all 1024 positions.
All inputs are finite; a program needn't handle non-finite values.
Results may differ from the reference program's by a relative error of at most 0.014.
The reference program's roundings to bfloat16 on the way count: a program that leaves them out, or rounds other values in their place, can miss the bound.
Values may be sent and summed in bfloat16 or wider, within the bound.
No kernel may reach another device: no remote copies, remote signals or barrier semaphores. Data moves between devices by JAX's collectives and lax.ppermute only.
A program may use at most 192 MiB of HBM per device.

```python
import math
import jax
import jax.numpy as jnp
import numpy as np
from jax import lax

D = 1024
FF = 2816
NH = 16
HK = 64
NG = 2
DV = 256
SPAN = 64
NDOM = 8
STEP = 10
LEN = 1024
SEQS = 8
QKVA = 1792
VALID = 6144


def draw_gate_bias(key, part):
    return jax.random.uniform(key, (NG * HK,), jnp.float32, -1.0, 12.0)


def with_ends(values, key, low, high):
    shape = values.shape
    spot = [jax.random.randint(jax.random.fold_in(key, axis), (), 0, shape[axis]) for axis in range(len(shape))]
    values = values.at[tuple(spot)].set(low)
    longest = shape.index(max(shape))
    spot[longest] = (spot[longest] + 1) % shape[longest]
    return values.at[tuple(spot)].set(high)


def level_of(own_key, shape, pieces, least, largest):
    loudness, own = 1.0, jax.random.fold_in(own_key, 6)
    for dim, parts in pieces:
        draws = jnp.exp(jax.random.uniform(jax.random.fold_in(own, dim), (parts,), jnp.float32, least / len(pieces), largest / len(pieces)))
        loudness = loudness * jnp.repeat(draws, shape[dim] // parts).reshape([-1 if axis == dim else 1 for axis in range(len(shape))])
    return loudness


def profile(count, total, reach, lean):
    portions = [(1 << 20) // math.isqrt(standing ** lean) + 1 for standing in range(2, count + 1)]
    spare, given = total - reach - (count - 1), [1] * (count - 1)
    while spare > 0:
        candidates = [i for i in range(count - 1) if given[i] < reach]
        whole, budget = sum([portions[i] for i in candidates]), spare
        for i in candidates:
            addition = min(reach - given[i], max(1, budget * portions[i] // whole), spare)
            given[i] = given[i] + addition
            spare = spare - addition
    return np.array([reach] + given)


def uneven(key, count, total, limit, slope):
    if count == 2:
        one = jax.random.randint(key, (), max(1, total - limit), min(limit, total - 1) + 1)
        return jnp.stack([one, total - one])
    tallies = jnp.asarray(profile(count, total, limit, slope), jnp.int32)
    pairs = (count - 1) // 2
    giver, taker = tallies[1:1 + 2 * pairs:2], tallies[2:2 + 2 * pairs:2]
    room = jnp.minimum(giver - 1, limit - taker)
    shifted = jax.random.randint(jax.random.fold_in(key, 1), (pairs,), 0, 1 << 20) % (room + 1)
    tallies = tallies.at[1:1 + 2 * pairs:2].set(giver - shifted).at[2:2 + 2 * pairs:2].set(taker + shifted)
    return tallies[jax.random.permutation(jax.random.fold_in(key, 2), count)]


def scatter_about(rng, shape, width, limit, cuts=(), held_as=jnp.bfloat16):
    level = level_of(rng, shape, cuts, -0.22, 0.18) if cuts else 1.0
    entries = jax.random.normal(rng, shape, jnp.float32) * width * level
    return jnp.minimum(jnp.maximum(entries, -limit), limit).astype(held_as)


def setup_inputs(seed: int = 0) -> dict:
    streams_of = jax.random.split(jax.random.key(seed), 24)
    return {
        "stream": scatter_about(streams_of[0], (SEQS, LEN, D), 1.0, 6.0, ((0, 8), (1, 4))),
        "cotangent": scatter_about(streams_of[1], (SEQS, LEN, D), 1.0, 6.0, ((0, 8), (1, 4))),
        "domains": with_ends(jax.random.randint(streams_of[2], (SEQS,), 0, NDOM), jax.random.fold_in(streams_of[2], 1), 0, NDOM - 1).astype(jnp.int32),
        "lengths": uneven(streams_of[3], SEQS, VALID, LEN, 1).astype(jnp.int32),
        "domain_weight": jnp.clip(jnp.exp(jax.random.uniform(streams_of[4], (NDOM,), jnp.float32, math.log(0.5), math.log(2.0))), 0.5, 2.0),
        "in_master": scatter_about(streams_of[5], (D, QKVA), D ** -0.5, 0.1875, ((0, 32),), jnp.float32),
        "in_first": scatter_about(streams_of[6], (D, QKVA), (0.22 * VALID ** 0.5), 112.0, ((0, 32),), jnp.float32),
        "in_second": jnp.clip(24.576 + 73.728 * jax.random.uniform(streams_of[7], (D, QKVA), jnp.float32) ** level_of(streams_of[7], (D, QKVA), ((0, 32),), -0.2, 0.2), 24.576, 98.304),
        "out_master": scatter_about(streams_of[8], (NH * DV, D), (NH * DV * LEN // 2) ** -0.5, 0.00390625, ((0, 32),), jnp.float32),
        "out_first": scatter_about(streams_of[9], (NH * DV, D), (0.078 * (LEN * VALID) ** 0.5), 1024.0, ((0, 32),), jnp.float32),
        "out_second": jnp.clip(3145.728 + 9437.184 * jax.random.uniform(streams_of[10], (NH * DV, D), jnp.float32) ** level_of(streams_of[10], (NH * DV, D), ((0, 32),), -0.2, 0.2), 3145.728, 12582.912),
        "gu_master": scatter_about(streams_of[11], (D, 2, FF), D ** -0.5, 0.1875, ((0, 8), (2, 4)), jnp.float32),
        "gu_first": scatter_about(streams_of[12], (D, 2, FF), (0.044 * VALID ** 0.5), 20.0, ((0, 8), (2, 4)), jnp.float32),
        "gu_second": jnp.clip(0.98304 + 2.94912 * jax.random.uniform(streams_of[13], (D, 2, FF), jnp.float32) ** level_of(streams_of[13], (D, 2, FF), ((0, 8), (2, 4)), -0.2, 0.2), 0.98304, 3.93216),
        "down_master": scatter_about(streams_of[14], (FF, D), FF ** -0.5, 0.109375, ((0, 4), (1, 8)), jnp.float32),
        "down_first": scatter_about(streams_of[15], (FF, D), (0.078 * VALID ** 0.5), 32.0, ((0, 4), (1, 8)), jnp.float32),
        "down_second": jnp.clip(3.01056 + 9.03168 * jax.random.uniform(streams_of[16], (FF, D), jnp.float32) ** level_of(streams_of[16], (FF, D), ((0, 4), (1, 8)), -0.2, 0.2), 3.01056, 12.04224),
        "gain_master": jnp.clip(1.0 + 0.1 * jax.random.normal(streams_of[17], (2, D), jnp.float32), 0.5, 1.5),
        "gain_first": scatter_about(streams_of[18], (2, D), (0.17 * VALID ** 0.5), 80.0, ((1, 32),), jnp.float32),
        "gain_second": jnp.clip(13.824 + 41.472 * jax.random.uniform(streams_of[19], (2, D), jnp.float32) ** level_of(streams_of[19], (2, D), ((1, 32),), -0.2, 0.2), 13.824, 55.296),
        "gate_bias": draw_gate_bias(jax.random.fold_in(streams_of[23], 71), 0),
        "bias_first": scatter_about(streams_of[21], (NG * HK,), (0.017 * VALID ** 0.5), 8.0, (), jnp.float32),
        "bias_second": jnp.clip(jax.random.uniform(streams_of[22], (NG * HK,), jnp.float32, 0.13824, 0.55296), 0.13824, 0.55296),
    }


NORM_EPS = 1e-05
GATE_NORM = 16.0
BETA_ONE = 0.9
BETA_TWO = 0.999
ADAM_EPS = 1e-06
WEIGHT_DECAY = 0.01
LEARN_RATE = 0.5
PRECISE = lax.Precision.HIGHEST

@jax.custom_vjp
def low(v):
    return lax.optimization_barrier(v.astype(jnp.bfloat16)).astype(jnp.float32)

@jax.custom_vjp
def low_back(v):
    return v

def low_keep(v):
    return (low(v), None)

def low_pass(kept, grad):
    return (grad,)

def back_keep(v):
    return (v, None)

def back_low(kept, grad):
    return (low(grad),)
low.defvjp(low_keep, low_pass)
low_back.defvjp(back_keep, back_low)

def mixer(queries, key_heads, values, gate_pre):
    batch_size, length, groups, per_group, key_width = queries.shape
    value_width = values.shape[-1]
    blocks = length // SPAN
    log_gate = jax.nn.log_sigmoid(gate_pre) / GATE_NORM
    query_blk = queries.reshape(batch_size, blocks, SPAN, groups, per_group, key_width) * key_width ** (-0.5)
    key_blk = key_heads.reshape(batch_size, blocks, SPAN, groups, key_width)
    value_blk = values.reshape(batch_size, blocks, SPAN, groups, value_width)
    cumulative = jnp.cumsum(log_gate.reshape(batch_size, blocks, SPAN, groups, key_width), axis=2)
    middle = cumulative[:, :, SPAN // 2:SPAN // 2 + 1]
    closing = cumulative[:, :, SPAN - 1:]
    query_mid = query_blk * jnp.exp(cumulative - middle)[:, :, :, :, None, :]
    key_mid = key_blk * jnp.exp(middle - cumulative)
    scores = jnp.einsum('bntgpc,bnsgc->bngpts', query_mid, key_mid, precision=PRECISE)
    causal = jnp.arange(SPAN)[:, None] >= jnp.arange(SPAN)[None, :]
    scores = jnp.where(causal, scores, 0.0)
    inner_part = jnp.einsum('bngpts,bnsgd->bntgpd', scores, value_blk, precision=PRECISE)
    key_last = key_blk * jnp.exp(closing - cumulative)
    adding = jnp.einsum('bnsgc,bnsgd->bngcd', key_last, value_blk, precision=PRECISE)
    shrink = jnp.exp(closing[:, :, 0])

    def advance(carried, step_item):
        factor, increment = step_item
        return (carried * factor[..., None] + increment, carried)
    initial = jnp.zeros((batch_size, groups, key_width, value_width), jnp.float32)
    unused, before = lax.scan(advance, initial, (jnp.moveaxis(shrink, 1, 0), jnp.moveaxis(adding, 1, 0)))
    before = jnp.moveaxis(before, 0, 1)
    query_abs = query_blk * jnp.exp(cumulative)[:, :, :, :, None, :]
    outer_part = jnp.einsum('bntgpc,bngcd->bntgpd', query_abs, before, precision=PRECISE)
    return (inner_part + outer_part).reshape(batch_size, length, groups, per_group, value_width)

def normalize(stream_f):
    inverse = lax.rsqrt(lax.optimization_barrier(jnp.mean(stream_f * stream_f, axis=-1, keepdims=True)) + NORM_EPS)
    return (stream_f * inverse, inverse)

def block_forward(weights, stream_f):
    w_in, w_out, w_gu, w_down, gain_rows = tuple((low(matrix) for matrix in weights[:5]))
    gate_bias = weights[5]
    query_end = NH * HK
    key_end = query_end + NG * HK
    value_end = key_end + NG * DV
    hat_one = normalize(stream_f)[0]
    normed_one = low(hat_one * gain_rows[0])
    projected = low_back(low(jnp.dot(normed_one, w_in, precision=PRECISE)))
    queries = projected[:, :query_end].reshape(1, LEN, NG, NH // NG, HK)
    key_heads = projected[:, query_end:key_end].reshape(1, LEN, NG, HK)
    values = projected[:, key_end:value_end].reshape(1, LEN, NG, DV)
    gate_pre = projected[:, value_end:].reshape(1, LEN, NG, HK) + gate_bias.reshape(NG, HK)
    mixed_heads = low_back(low(mixer(queries, key_heads, values, gate_pre).reshape(LEN, NH * DV)))
    attended = low_back(jnp.dot(mixed_heads, w_out, precision=PRECISE))
    middle = stream_f + attended
    hat_two = normalize(middle)[0]
    normed_two = low(hat_two * gain_rows[1])
    gate_up = low_back(jnp.einsum('td,dkf->tkf', normed_two, w_gu, precision=PRECISE))
    hidden = low(jax.nn.silu(gate_up[:, 0]) * gate_up[:, 1])
    branch = low_back(jnp.dot(hidden, w_down, precision=PRECISE))
    return (middle + branch, attended, branch)

def piece_squares(in_w, out_w, gu_w, down_w, gain_w):
    query_end = NH * HK
    key_end = query_end + NG * HK
    value_end = key_end + NG * DV
    columns = lax.optimization_barrier(jnp.sum(in_w * in_w, axis=0))
    first_four = jnp.stack([jnp.sum(columns[:query_end]), jnp.sum(columns[query_end:key_end]), jnp.sum(columns[key_end:value_end]), jnp.sum(columns[value_end:])])
    return jnp.concatenate([first_four, jnp.sum(out_w * out_w)[None], lax.optimization_barrier(jnp.sum(gu_w * gu_w, axis=(0, 2))), jnp.sum(down_w * down_w)[None], lax.optimization_barrier(jnp.sum(gain_w * gain_w, axis=1))])

def moments(weight, first_old, second_old, gradient):
    first_new = BETA_ONE * first_old + (1.0 - BETA_ONE) * gradient
    second_new = BETA_TWO * second_old + (1.0 - BETA_TWO) * gradient * gradient
    update = first_new / (1.0 - BETA_ONE ** STEP) / (jnp.sqrt(second_new / (1.0 - BETA_TWO ** STEP)) + ADAM_EPS) + WEIGHT_DECAY * weight
    return (first_new, second_new, update)

def apply_ratio(trust_ratio, in_w, in_u, out_w, out_u, gu_w, gu_u, down_w, down_u, gain_w, gain_u):
    column_ratio = jnp.concatenate([jnp.full((NH * HK,), trust_ratio[0]), jnp.full((NG * HK,), trust_ratio[1]), jnp.full((NG * DV,), trust_ratio[2]), jnp.full((NG * HK,), trust_ratio[3])])
    return (in_w - LEARN_RATE * column_ratio[None, :] * in_u, out_w - LEARN_RATE * trust_ratio[4] * out_u, gu_w - LEARN_RATE * trust_ratio[5:7][None, :, None] * gu_u, down_w - LEARN_RATE * trust_ratio[7] * down_u, gain_w - LEARN_RATE * trust_ratio[8:10][:, None] * gain_u)

def reference(stream, cotangent, domains, lengths, domain_weight, in_master, in_first, in_second, out_master, out_first, out_second, gu_master, gu_first, gu_second, down_master, down_first, down_second, gain_master, gain_first, gain_second, gate_bias, bias_first, bias_second):
    positions = jnp.arange(LEN)
    valid_mask = (positions[None, :] < lengths[:, None]).astype(jnp.float32)
    picked = domains[:, None] == jnp.arange(NDOM)[None, :]
    seq_weight = lax.optimization_barrier(jnp.sum(jnp.where(picked, domain_weight[None, :], 0.0), axis=1))
    row_scale = valid_mask * seq_weight[:, None]
    grad_eff = cotangent.astype(jnp.float32) * row_scale[:, :, None]
    params = (in_master, out_master, gu_master, down_master, gain_master, gate_bias)

    def all_sequences(weights, streams):

        def one_seq(totals, pair_in):
            stream_f, mask_row = pair_in
            result, attended, branch = block_forward(weights, stream_f)
            mask_wide = mask_row[:, None]
            partial_value = jnp.stack([jnp.sum(mask_wide * stream_f * stream_f), jnp.sum(mask_wide * attended * attended), jnp.sum(mask_wide * branch * branch)])
            return (totals + partial_value, result)
        totals, results = lax.scan(jax.checkpoint(one_seq), jnp.zeros((3,), jnp.float32), (streams, valid_mask))
        return (results, totals)
    results, backward, totals = jax.vjp(all_sequences, params, stream.astype(jnp.float32), has_aux=True)
    gradients, grad_stream = backward(grad_eff)
    in_first_new, in_second_new, in_update = moments(in_master, in_first, in_second, gradients[0])
    out_first_new, out_second_new, out_update = moments(out_master, out_first, out_second, gradients[1])
    gu_first_new, gu_second_new, gu_update = moments(gu_master, gu_first, gu_second, gradients[2])
    down_first_new, down_second_new, down_update = moments(down_master, down_first, down_second, gradients[3])
    gain_first_new, gain_second_new, gain_update = moments(gain_master, gain_first, gain_second, gradients[4])
    bias_first_new, bias_second_new, bias_update = moments(gate_bias, bias_first, bias_second, gradients[5])
    weight_norm = jnp.concatenate([jnp.sqrt(piece_squares(in_master, out_master, gu_master, down_master, gain_master)), jnp.sqrt(jnp.sum(gate_bias * gate_bias))[None]])
    update_norm = jnp.concatenate([jnp.sqrt(piece_squares(in_update, out_update, gu_update, down_update, gain_update)), jnp.sqrt(jnp.sum(bias_update * bias_update))[None]])
    trust_ratio = weight_norm / update_norm
    in_new, out_new, gu_new, down_new, gain_new = apply_ratio(trust_ratio, in_master, in_update, out_master, out_update, gu_master, gu_update, down_master, down_update, gain_master, gain_update)
    bias_new = gate_bias - LEARN_RATE * trust_ratio[10] * bias_update
    valid_count = jnp.sum(lengths).astype(jnp.float32)
    stream_stats = jnp.sqrt(totals / (valid_count * D))
    norm_table = jnp.stack([weight_norm, update_norm])
    return (results.astype(jnp.bfloat16), grad_stream.astype(jnp.bfloat16), in_new, in_first_new, in_second_new, out_new, out_first_new, out_second_new, gu_new, gu_first_new, gu_second_new, down_new, down_first_new, down_second_new, gain_new, gain_first_new, gain_second_new, bias_new, bias_first_new, bias_second_new, norm_table, stream_stats)
```

```python
import jax
import jax.numpy as jnp
from jax import lax
from jax.sharding import PartitionSpec as P

NH = 16
HK = 64
NG = 2
DV = 256
SPAN = 64
NDOM = 8
STEP = 10

NORM_EPS = 1e-05
GATE_NORM = 16.0
BETA_ONE = 0.9
BETA_TWO = 0.999
ADAM_EPS = 1e-06
WEIGHT_DECAY = 0.01
LEARN_RATE = 0.5
PRECISE = lax.Precision.HIGHEST


BF = jnp.bfloat16
F32 = jnp.float32
ALL = ("seq", "dp")


def xor_pairs(count, mask):
    return [(i, i ^ mask) for i in range(count)]


def swap(x, axis, mask):
    return lax.ppermute(x, axis, xor_pairs(lax.axis_size(axis), mask))


def gather_seq(x):
    return [x] + [swap(x, "seq", j) for j in range(1, lax.axis_size("seq"))]


def scatter_seq(parts):
    total = parts[0]
    got = [swap(parts[j].astype(BF), "seq", j) for j in range(1, len(parts))]
    for piece in got:
        total = total + piece.astype(F32)
    return total


def ordered(pieces, rank):
    count = len(pieces)
    mask = 1
    while mask < count:
        bit = (rank & mask) != 0
        pieces = [
            jnp.where(bit, pieces[i ^ mask], pieces[i]) for i in range(count)
        ]
        mask *= 2
    return pieces


def gather_dp(x):
    count = lax.axis_size("dp")
    if count > 8:
        everything = lax.all_gather(x, "dp", axis=0)
        return [everything[i] for i in range(count)]
    rank = lax.axis_index("dp")
    mine = [x] + [swap(x, "dp", 2 * k) for k in range(1, count // 2)]
    mine = jnp.stack(ordered(mine, rank // 2))
    other = swap(mine, "dp", 1)
    odd = (rank & 1) != 0
    even_part = jnp.where(odd, other, mine)
    odd_part = jnp.where(odd, mine, other)
    return [(odd_part if i & 1 else even_part)[i // 2] for i in range(count)]


def scatter_dp(g):
    count = lax.axis_size("dp")
    if count > 8:
        got = lax.all_to_all(g.astype(BF), "dp", split_axis=0, concat_axis=0, tiled=True)
        return jnp.sum(got.astype(F32), axis=0)
    rank = lax.axis_index("dp")
    outer, inner = rank // 2, rank & 1
    pairs = g.reshape((count // 2, 2) + g.shape[1:])
    keep = lax.dynamic_index_in_dim(pairs, inner, 1, keepdims=False)
    give = lax.dynamic_index_in_dim(pairs, 1 - inner, 1, keepdims=False)
    half = keep + swap(give.astype(BF), "dp", 1).astype(F32)
    total = lax.dynamic_index_in_dim(half, outer, 0, keepdims=False)
    sends = [
        lax.dynamic_index_in_dim(half, outer ^ k, 0, keepdims=False).astype(BF)
        for k in range(1, count // 2)
    ]
    for k, piece in enumerate(sends):
        total = total + swap(piece, "dp", 2 * (k + 1)).astype(F32)
    return total


def after(x, *others):
    return lax.optimization_barrier((x,) + others)[0]


def mixer(queries, key_heads, values, gate_pre):
    batch_size, length, groups, per_group, key_width = queries.shape
    value_width = values.shape[-1]
    blocks = length // SPAN
    log_gate = jax.nn.log_sigmoid(gate_pre) / GATE_NORM
    query_blk = queries.reshape(
        batch_size, blocks, SPAN, groups, per_group, key_width
    ) * key_width ** (-0.5)
    key_blk = key_heads.reshape(batch_size, blocks, SPAN, groups, key_width)
    value_blk = values.reshape(batch_size, blocks, SPAN, groups, value_width)
    cumulative = jnp.cumsum(log_gate.reshape(batch_size, blocks, SPAN, groups, key_width), axis=2)
    middle = cumulative[:, :, SPAN // 2 : SPAN // 2 + 1]
    closing = cumulative[:, :, SPAN - 1 :]
    query_mid = query_blk * jnp.exp(cumulative - middle)[:, :, :, :, None, :]
    key_mid = key_blk * jnp.exp(middle - cumulative)
    scores = jnp.einsum("bntgpc,bnsgc->bngpts", query_mid, key_mid, precision=PRECISE)
    causal = jnp.arange(SPAN)[:, None] >= jnp.arange(SPAN)[None, :]
    scores = jnp.where(causal, scores, 0.0)
    inner_part = jnp.einsum("bngpts,bnsgd->bntgpd", scores, value_blk, precision=PRECISE)
    key_last = key_blk * jnp.exp(closing - cumulative)
    adding = jnp.einsum("bnsgc,bnsgd->bngcd", key_last, value_blk, precision=PRECISE)
    shrink = jnp.exp(closing[:, :, 0])

    def advance(carried, step_item):
        factor, increment = step_item
        return (carried * factor[..., None] + increment, carried)

    initial = jnp.zeros((batch_size, groups, key_width, value_width), F32)
    unused, before = lax.scan(
        advance, initial, (jnp.moveaxis(shrink, 1, 0), jnp.moveaxis(adding, 1, 0))
    )
    before = jnp.moveaxis(before, 0, 1)
    query_abs = query_blk * jnp.exp(cumulative)[:, :, :, :, None, :]
    outer_part = jnp.einsum("bntgpc,bngcd->bntgpd", query_abs, before, precision=PRECISE)
    return (inner_part + outer_part).reshape(batch_size, length, groups, per_group, value_width)


def normalize(stream_f):
    inverse = lax.rsqrt(jnp.mean(stream_f * stream_f, axis=-1, keepdims=True) + NORM_EPS)
    return (stream_f * inverse, inverse)


def norm_back(grad_normed, hat_value, inverse, gain_row):
    grad_hat = grad_normed * gain_row
    return inverse * (grad_hat - hat_value * jnp.mean(grad_hat * hat_value, axis=-1, keepdims=True))


def dot(a, b, dims):
    return lax.dot_general(a, b, (dims, ((), ())), preferred_element_type=F32)


def mm(a, b):
    return dot(a, b, ((1,), (0,)))


def mm_nt(a, b):
    return dot(a, b, ((1,), (1,)))


def mm_tn(a, b):
    return dot(a, b, ((0,), (0,)))


def piece_squares(in_w, out_w, gu_w, down_w, gain_w):
    query_end = NH * HK
    key_end = query_end + NG * HK
    value_end = key_end + NG * DV
    columns = jnp.sum(in_w * in_w, axis=0)
    first_four = jnp.stack(
        [
            jnp.sum(columns[:query_end]),
            jnp.sum(columns[query_end:key_end]),
            jnp.sum(columns[key_end:value_end]),
            jnp.sum(columns[value_end:]),
        ]
    )
    return jnp.concatenate(
        [
            first_four,
            jnp.sum(out_w * out_w)[None],
            jnp.sum(gu_w * gu_w, axis=(0, 2)),
            jnp.sum(down_w * down_w)[None],
            jnp.sum(gain_w * gain_w, axis=1),
        ]
    )


def moments(weight, first_old, second_old, gradient):
    first_new = BETA_ONE * first_old + (1.0 - BETA_ONE) * gradient
    second_new = BETA_TWO * second_old + (1.0 - BETA_TWO) * gradient * gradient
    update = (
        first_new
        / (1.0 - BETA_ONE**STEP)
        / (jnp.sqrt(second_new / (1.0 - BETA_TWO**STEP)) + ADAM_EPS)
        + WEIGHT_DECAY * weight
    )
    return (first_new, second_new, update)


def apply_ratio(trust_ratio, in_w, in_u, out_w, out_u, gu_w, gu_u, down_w, down_u, gain_w, gain_u):
    column_ratio = jnp.concatenate(
        [
            jnp.full((NH * HK,), trust_ratio[0]),
            jnp.full((NG * HK,), trust_ratio[1]),
            jnp.full((NG * DV,), trust_ratio[2]),
            jnp.full((NG * HK,), trust_ratio[3]),
        ]
    )
    return (
        in_w - LEARN_RATE * column_ratio[None, :] * in_u,
        out_w - LEARN_RATE * trust_ratio[4] * out_u,
        gu_w - LEARN_RATE * trust_ratio[5:7][None, :, None] * gu_u,
        down_w - LEARN_RATE * trust_ratio[7] * down_u,
        gain_w - LEARN_RATE * trust_ratio[8:10][:, None] * gain_u,
    )


def shards(
    stream,
    cotangent,
    domains,
    lengths,
    domain_weight,
    in_master,
    in_first,
    in_second,
    out_master,
    out_first,
    out_second,
    gu_master,
    gu_first,
    gu_second,
    down_master,
    down_first,
    down_second,
    gain_master,
    gain_first,
    gain_second,
    gate_bias,
    bias_first,
    bias_second,
):
    seq_count = lax.axis_size("seq")
    dp_count = lax.axis_size("dp")
    everyone = seq_count * dp_count
    seq_rank = lax.axis_index("seq")
    dp_rank = lax.axis_index("dp")
    one_seq, tok_local, width = stream.shape
    length = tok_local * seq_count
    heads = NH // seq_count
    repeats = seq_count // NG
    group = seq_rank // repeats
    query_end = NH * HK
    key_end = query_end + NG * HK
    value_end = key_end + NG * DV
    in_rows = in_master.shape[0]
    hidden_units = down_master.shape[0]

    stream_pieces = gather_seq(stream[0])
    gain_local = gain_master.astype(BF)
    gain_send = jnp.broadcast_to(gain_local.astype(F32).reshape(1, -1), (everyone, gain_local.size))
    gain_got = lax.all_to_all(gain_send, ALL, split_axis=0, concat_axis=0, tiled=True)
    gain_all = jnp.swapaxes(gain_got.reshape(everyone, 2, -1), 0, 1).reshape(2, width)
    gain_one, gain_two = gain_all[0], gain_all[1]

    in_low = in_master.astype(BF)

    def own_columns(s):
        g = s // repeats
        return jnp.concatenate(
            [
                in_low[:, s * heads * HK : (s + 1) * heads * HK],
                in_low[:, key_end + g * DV : key_end + (g + 1) * DV],
                in_low[:, query_end + g * HK : query_end + (g + 1) * HK],
                in_low[:, value_end + g * HK : value_end + (g + 1) * HK],
            ],
            axis=1,
        )

    own_width = heads * HK + DV + 2 * HK
    by_rank = ordered([own_columns(s) for s in range(seq_count)], seq_rank)
    in_seq = [by_rank[0]] + [swap(by_rank[j], "seq", j) for j in range(1, seq_count)]
    in_seq = jnp.stack(ordered(in_seq, seq_rank))
    w_in = jnp.stack(gather_dp(in_seq), axis=1).reshape(width, own_width)

    w_out = jnp.concatenate(gather_dp(after(out_master.astype(BF), w_in)), axis=0)
    gu_low = jnp.swapaxes(gu_master.astype(BF), 0, 1)
    w_gu = jnp.concatenate(gather_dp(after(gu_low, w_out)), axis=1)
    w_down = jnp.concatenate(gather_dp(after(down_master.astype(BF), w_out)), axis=1)

    my_length = lengths[dp_rank]
    picked = domains[dp_rank] == jnp.arange(NDOM)
    seq_weight = jnp.sum(jnp.where(picked, domain_weight, 0.0))
    positions = seq_rank * tok_local + jnp.arange(tok_local)
    valid_mask = (positions < my_length).astype(F32)
    row_scale = valid_mask * seq_weight
    grad_eff = cotangent[0].astype(F32) * row_scale[:, None]
    grad_branch = grad_eff.astype(BF)

    stream_f = stream[0].astype(F32)
    stream_all = jnp.concatenate(stream_pieces, axis=0).astype(F32)
    hat_all, inverse_all = normalize(stream_all)
    normed_one = (hat_all * gain_one).astype(BF)
    projected = mm(normed_one, w_in).astype(BF)

    def reorder(x):
        x = x.reshape((seq_count, tok_local) + x.shape[1:])
        x = jnp.stack(ordered([x[j] for j in range(seq_count)], seq_rank))
        return x.reshape((length,) + x.shape[2:])

    projected_abs = reorder(projected).astype(F32)
    q_end = heads * HK
    v_end = q_end + DV
    queries = projected_abs[:, :q_end].reshape(1, length, 1, heads, HK)
    values = projected_abs[:, q_end:v_end].reshape(1, length, 1, DV)
    key_heads = projected_abs[:, v_end : v_end + HK].reshape(1, length, 1, HK)
    bias_group = lax.dynamic_slice_in_dim(gate_bias.reshape(NG, HK), group, 1)
    gate_pre = projected_abs[:, v_end + HK :].reshape(1, length, 1, HK) + bias_group
    mixed_abs, mixer_back = jax.vjp(mixer, queries, key_heads, values, gate_pre)
    mixed = reorder(mixed_abs.reshape(length, heads * DV).astype(BF))

    def pieces_of(x):
        return [x[j * tok_local : (j + 1) * tok_local] for j in range(seq_count)]

    attended = scatter_seq(pieces_of(mm(mixed, w_out)))
    middle = stream_f + attended
    hat_two, inverse_two = normalize(middle)
    normed_two = (hat_two * gain_two).astype(BF)

    normed_two_all = jnp.concatenate(gather_seq(normed_two), axis=0)
    grad_branch_all = jnp.concatenate(gather_seq(after(grad_branch, projected)), axis=0)
    gate_value = mm(normed_two_all, w_gu[0])
    up_value = mm(normed_two_all, w_gu[1])
    sigmoid_gate = jax.nn.sigmoid(gate_value)
    silu_gate = gate_value * sigmoid_gate
    hidden = (silu_gate * up_value).astype(BF)
    grad_hidden = mm_nt(grad_branch_all, w_down)
    grad_gate = (
        grad_hidden * up_value * sigmoid_gate * (1.0 + gate_value * (1.0 - sigmoid_gate))
    ).astype(BF)
    grad_up = (grad_hidden * silu_gate).astype(BF)
    grad_two_part = mm_nt(grad_gate, w_gu[0]) + mm_nt(grad_up, w_gu[1])
    grad_normed_two = scatter_seq(pieces_of(grad_two_part))
    branch = scatter_seq(pieces_of(mm(hidden, w_down)))
    grad_down = mm_tn(hidden, grad_branch_all)
    grad_gu = jnp.stack([mm_tn(normed_two_all, grad_gate), mm_tn(normed_two_all, grad_up)])

    output = (middle + branch).astype(BF)
    mask_wide = valid_mask[:, None]
    stat_sums = jnp.stack(
        [
            jnp.sum(mask_wide * stream_f * stream_f),
            jnp.sum(mask_wide * attended * attended),
            jnp.sum(mask_wide * branch * branch),
        ]
    )
    grad_middle = grad_eff + norm_back(grad_normed_two, hat_two, inverse_two, gain_two)
    grad_gain_two = jnp.sum(grad_normed_two * hat_two, axis=0)

    grad_attended_all = jnp.concatenate(gather_seq(grad_middle.astype(BF)), axis=0)
    grad_mixed = mm_nt(grad_attended_all, w_out).astype(BF)
    grad_w_out = mm_tn(mixed, grad_attended_all)
    grad_q, grad_k, grad_v, grad_g = mixer_back(
        reorder(grad_mixed).astype(F32).reshape(1, length, 1, heads, DV)
    )
    bias_own = jnp.sum(grad_g, axis=(0, 1)).reshape(HK)
    grad_projected = reorder(
        jnp.concatenate(
            [
                grad_q.reshape(length, heads * HK),
                grad_v.reshape(length, DV),
                grad_k.reshape(length, HK),
                grad_g.reshape(length, HK),
            ],
            axis=1,
        ).astype(BF)
    )
    grad_w_in = mm_tn(normed_one, grad_projected)
    grad_one_part = mm_nt(grad_projected, w_in)
    grad_gain_one = jnp.sum(grad_one_part * hat_all, axis=0)
    grad_normed_one = scatter_seq(pieces_of(grad_one_part))
    hat_one, inverse_one = normalize(stream_f)
    grad_stream = (grad_middle + norm_back(grad_normed_one, hat_one, inverse_one, gain_one)).astype(BF)

    sum_gu = jnp.swapaxes(
        scatter_dp(jnp.swapaxes(grad_gu.reshape(2, dp_count, -1, hidden_units), 0, 1)), 0, 1
    )
    sum_down = scatter_dp(jnp.swapaxes(grad_down.reshape(hidden_units, dp_count, -1), 0, 1))
    sum_out = scatter_dp(grad_w_out.reshape(dp_count, -1, width))
    in_sum = scatter_dp(
        jnp.swapaxes(grad_w_in.reshape(seq_count, dp_count, in_rows, own_width), 0, 1)
    )
    in_send = ordered([in_sum[s].astype(BF) for s in range(seq_count)], seq_rank)
    in_got = [in_send[0]] + [swap(in_send[j], "seq", j) for j in range(1, seq_count)]
    in_got = [piece.astype(F32) for piece in ordered(in_got, seq_rank)]

    def group_sum(lo, hi):
        return [
            sum(in_got[g * repeats + r][:, lo:hi] for r in range(repeats)) for g in range(NG)
        ]

    sum_in = jnp.concatenate(
        [piece[:, :q_end] for piece in in_got]
        + group_sum(v_end, v_end + HK)
        + group_sum(q_end, v_end)
        + group_sum(v_end + HK, own_width),
        axis=1,
    )

    bias_part = jnp.where(jnp.arange(NG)[:, None] == group, bias_own[None, :], 0.0).reshape(NG * HK)
    weight_sq = piece_squares(in_master, out_master, gu_master, down_master, gain_master)
    gain_cols = jnp.stack([grad_gain_one, grad_gain_two])
    gain_send = jnp.swapaxes(gain_cols.reshape(2, everyone, -1), 0, 1).reshape(everyone, -1)
    gain_width = gain_send.shape[1]
    common = jnp.concatenate([bias_part, weight_sq, stat_sums])
    small = jnp.concatenate(
        [gain_send, jnp.broadcast_to(common[None], (everyone, common.shape[0]))], axis=1
    )
    small = jnp.sum(
        lax.all_to_all(small, ALL, split_axis=0, concat_axis=0, tiled=True), axis=0
    )
    sum_gains = small[:gain_width].reshape(2, -1)
    bias_grad = small[gain_width : gain_width + NG * HK]
    weight_tot = small[gain_width + NG * HK : gain_width + NG * HK + 10]
    stat_tot = small[gain_width + NG * HK + 10 :]

    in_first_new, in_second_new, in_update = moments(in_master, in_first, in_second, sum_in)
    out_first_new, out_second_new, out_update = moments(out_master, out_first, out_second, sum_out)
    gu_first_new, gu_second_new, gu_update = moments(gu_master, gu_first, gu_second, sum_gu)
    down_first_new, down_second_new, down_update = moments(
        down_master, down_first, down_second, sum_down
    )
    gain_first_new, gain_second_new, gain_update = moments(
        gain_master, gain_first, gain_second, sum_gains
    )
    update_sq = piece_squares(in_update, out_update, gu_update, down_update, gain_update)
    update_all = lax.all_to_all(
        jnp.broadcast_to(update_sq[None], (everyone, 10)), ALL, split_axis=0, concat_axis=0, tiled=True
    )
    update_tot = jnp.sum(update_all, axis=0)
    bias_first_new, bias_second_new, bias_update = moments(
        gate_bias, bias_first, bias_second, bias_grad
    )
    weight_norm = jnp.concatenate(
        [jnp.sqrt(weight_tot), jnp.sqrt(jnp.sum(gate_bias * gate_bias))[None]]
    )
    update_norm = jnp.concatenate(
        [jnp.sqrt(update_tot), jnp.sqrt(jnp.sum(bias_update * bias_update))[None]]
    )
    trust_ratio = weight_norm / update_norm
    in_new, out_new, gu_new, down_new, gain_new = apply_ratio(
        trust_ratio,
        in_master,
        in_update,
        out_master,
        out_update,
        gu_master,
        gu_update,
        down_master,
        down_update,
        gain_master,
        gain_update,
    )
    bias_new = gate_bias - LEARN_RATE * trust_ratio[10] * bias_update
    valid_count = jnp.sum(lengths).astype(F32)
    stream_stats = jnp.sqrt(stat_tot / (valid_count * width))
    norm_table = jnp.stack([weight_norm, update_norm])
    return (
        output[None],
        grad_stream[None],
        in_new,
        in_first_new,
        in_second_new,
        out_new,
        out_first_new,
        out_second_new,
        gu_new,
        gu_first_new,
        gu_second_new,
        down_new,
        down_first_new,
        down_second_new,
        gain_new,
        gain_first_new,
        gain_second_new,
        bias_new,
        bias_first_new,
        bias_second_new,
        norm_table,
        stream_stats,
    )


def solution(mesh):
    rows = P(ALL, None)
    gu = P("dp", None, "seq")
    down = P("seq", "dp")
    gain = P(None, ALL)
    tokens = P("dp", "seq", None)
    return jax.shard_map(
        shards,
        mesh=mesh,
        in_specs=(tokens, tokens, P(), P(), P())
        + (rows,) * 6
        + (gu,) * 3
        + (down,) * 3
        + (gain,) * 3
        + (P(),) * 3,
        out_specs=(tokens, tokens)
        + (rows,) * 6
        + (gu,) * 3
        + (down,) * 3
        + (gain,) * 3
        + (P(),) * 5,
        check_vma=False,
    )
```
